256 devices in a mesh: grp: 4 (over y), dom: 64 (over x, z, core).
Axes of the slice: x: 4, y: 4, z: 8, core: 2. Of those that a mesh axis runs over, the one named last changes fastest.
Arguments:
- features: bfloat16 [786432, 256], P(('grp', 'dom')), may hold values from -6 to 6
- boundary_cache: float32 [65536, 256], P(('grp', 'dom')), may hold values from -6 to 6
- adjacency: bfloat16 [6144, 2, 128, 128], P(('grp', 'dom')), may hold values from -0.375 to 0.375
- neighbor: int32 [6144, 2], P(('grp', 'dom')), may hold values from 0 to 87
- counts: int32 [6144], P(('grp', 'dom')), may hold values from 1 to 2
- wanted: int32 [256, 64], P(('grp', 'dom')), may hold values from 0 to 1
- weight_in: bfloat16 [512, 512], replicated, may hold values from -0.25 to 0.25
- weight_out: bfloat16 [512, 256], replicated, may hold values from -0.25 to 0.25
- cotangent: bfloat16 [786432, 256], P(('grp', 'dom')), may hold values from -6 to 6
Outputs:
- grad_features: bfloat16 [786432, 256], P(('grp', 'dom'))
- grad_weight_in: float32 [512, 512], P('dom')
- grad_weight_out: float32 [512, 256], P('dom')
The draws below stay inside these ranges and needn't reach their ends.
Inputs may be any that keep to these rules, and one draw needn't show every extreme that they name: `neighbor`: A value under 24 names a block of the same partition; a value 24 + q names the boundary block that the partition reads from partition q of its group. Slots from counts[b] on are padding and carry no edges.
All inputs are finite; a program needn't handle non-finite values.
Results may differ from the reference program's by a relative error of at most 0.0054.
Values may be sent and summed in bfloat16 or wider, within the bound.
No kernel may reach another device: no remote copies, remote signals or barrier semaphores. Data moves between devices by JAX's collectives and lax.ppermute only.
A program may use at most 128 MiB of HBM per device.

```python
import jax
import jax.numpy as jnp
from jax import lax

F = 256
HID = 512
BLK = 128
S = 2
E = 2
NB_DEV = 24
NODES = 786432
N_GRP = 4
N_DOM = 64


def touch_ends(result, rng, low, high):
    longest = result.shape.index(max(result.shape))
    spots = []
    for shift in (0, 1):
        where = [jax.random.randint(jax.random.fold_in(rng, axis), (), 0, length) for axis, length in enumerate(result.shape)]
        where[longest] = (where[longest] + shift) % result.shape[longest]
        spots.append(tuple(where))
    return result.at[spots[0]].set(low).at[spots[1]].set(high)


def levels(stream_key, extent, split, smallest, top_value):
    factor_of = 1.0
    for axis_at, blocks in split:
        heights = jax.random.uniform(jax.random.fold_in(jax.random.fold_in(stream_key, 6), axis_at), (blocks,), jnp.float32, smallest / len(split), top_value / len(split))
        factor_of = factor_of * jnp.repeat(jnp.exp(heights), extent[axis_at] // blocks).reshape((-1,) + (1,) * (len(extent) - 1 - axis_at))
    return factor_of


def noise(key, shape, scale, limit, pieces=(), held_as=jnp.bfloat16):
    drawn = jax.random.normal(key, shape, jnp.float32) * scale
    if len(pieces) > 0:
        drawn = levels(key, shape, pieces, -0.22, 0.18) * drawn
    return jnp.clip(drawn, min=-limit, max=limit).astype(held_as)


def setup_inputs(seed: int = 0) -> dict:
    arg_keys = jax.random.split(jax.random.key(seed), 10)
    return {
        "features": noise(arg_keys[0], (NODES, F), 1.0, 6.0, ((0, 256),)),
        "boundary_cache": noise(arg_keys[1], (E * BLK * N_GRP * N_DOM, F), 1.0, 6.0, ((0, 256),), jnp.float32),
        "adjacency": noise(arg_keys[2], (NB_DEV * N_GRP * N_DOM, S, BLK, BLK), (BLK * S) ** -0.5, 0.375, ((0, 256),)),
        "neighbor": touch_ends(jax.random.randint(arg_keys[3], (NB_DEV * N_GRP * N_DOM, S), 0, NB_DEV + N_DOM), jax.random.fold_in(arg_keys[3], 1), 0, (NB_DEV + N_DOM) - 1).astype(jnp.int32),
        "counts": touch_ends(jax.random.randint(arg_keys[4], (NB_DEV * N_GRP * N_DOM,), 1, S + 1), jax.random.fold_in(arg_keys[4], 1), 1, S).astype(jnp.int32),
        "wanted": touch_ends(jax.random.randint(arg_keys[5], (N_GRP * N_DOM, N_DOM), 0, E), jax.random.fold_in(arg_keys[5], 1), 0, E - 1).astype(jnp.int32),
        "weight_in": noise(arg_keys[6], (2 * F, HID), (2 * F) ** -0.5, 0.25),
        "weight_out": noise(arg_keys[7], (HID, F), HID ** -0.5, 0.25),
        "cotangent": noise(arg_keys[8], (NODES, F), 1.0, 6.0, ((0, 256),)),
    }


def partition_grads(features_p, adjacency_p, neighbor_p, counts_p, wanted_p, cotangent_p, group_cache, weight_in, weight_out):
    block_rows = adjacency_p.shape[2]
    nblocks = adjacency_p.shape[0]
    slot_total = adjacency_p.shape[1]
    channels = features_p.shape[1]
    boundary = jnp.take_along_axis(group_cache, wanted_p[:, None, None, None], axis=1)[:, 0]
    owned = features_p.reshape(nblocks, block_rows, channels)
    sources = jnp.concatenate([owned, boundary], 0)
    active = jnp.arange(slot_total)[None, :] < counts_p[:, None]
    chosen = sources[neighbor_p]
    chosen = jnp.where(active[:, :, None, None], chosen, jnp.zeros_like(chosen))
    aggregate = jnp.einsum("bsij,bsjf->bif", adjacency_p.astype(jnp.float32), chosen.astype(jnp.float32))
    aggregate = aggregate.astype(jnp.bfloat16).reshape(nblocks * block_rows, channels)
    joined = jnp.concatenate([aggregate, features_p], 1)
    preact = jnp.dot(joined, weight_in, preferred_element_type=jnp.float32)
    gating = jax.nn.sigmoid(preact)
    hidden = (preact * gating).astype(jnp.bfloat16)
    grad_hidden = jnp.dot(cotangent_p, weight_out.T, preferred_element_type=jnp.float32)
    grad_preact = (grad_hidden * gating * (1.0 + preact * (1.0 - gating))).astype(jnp.bfloat16)
    grad_joined = jnp.dot(grad_preact, weight_in.T, preferred_element_type=jnp.float32)
    grad_aggregate = grad_joined[:, :channels].astype(jnp.bfloat16).reshape(nblocks, block_rows, channels)
    backward = jnp.einsum("bsji,bjf->bsif", adjacency_p.astype(jnp.float32), grad_aggregate.astype(jnp.float32))
    local_hit = active & (neighbor_p < nblocks)
    routing = (neighbor_p[None, :, :] == jnp.arange(nblocks)[:, None, None]) & local_hit[None]
    spread = jnp.einsum("cbs,bsif->cif", routing.astype(jnp.float32), backward, precision=lax.Precision.HIGHEST)
    grad_features = (grad_joined[:, channels:] + spread.reshape(nblocks * block_rows, channels)).astype(jnp.bfloat16)
    term_in = jnp.dot(joined.T.astype(jnp.float32), grad_preact.astype(jnp.float32), precision=lax.Precision.HIGHEST)
    term_out = jnp.dot(hidden.T.astype(jnp.float32), cotangent_p.astype(jnp.float32), precision=lax.Precision.HIGHEST)
    return grad_features, term_in, term_out


def reference(features, boundary_cache, adjacency, neighbor, counts, wanted, weight_in, weight_out, cotangent):
    parts = N_GRP * N_DOM
    cache_copy = boundary_cache.astype(jnp.bfloat16).reshape(N_GRP, N_DOM, E, BLK, F)
    features_all = features.reshape(parts, NB_DEV * BLK, F)
    cotangent_all = cotangent.reshape(parts, NB_DEV * BLK, F)
    adjacency_all = adjacency.reshape(parts, NB_DEV, S, BLK, BLK)
    neighbor_all = neighbor.reshape(parts, NB_DEV, S)
    counts_all = counts.reshape(parts, NB_DEV)
    groups = (jnp.arange(parts) // N_DOM).astype(jnp.int32)

    def step(carry, inputs):
        features_p, adjacency_p, neighbor_p, counts_p, wanted_p, cotangent_p, group = inputs
        group_cache = lax.dynamic_index_in_dim(cache_copy, group, 0, keepdims=False)
        grad_features, term_in, term_out = partition_grads(features_p, adjacency_p, neighbor_p, counts_p, wanted_p, cotangent_p, group_cache, weight_in, weight_out)
        return (carry[0] + term_in, carry[1] + term_out), grad_features

    start_sums = (jnp.zeros((2 * F, HID), jnp.float32), jnp.zeros((HID, F), jnp.float32))
    sums, grad_features = lax.scan(step, start_sums, (features_all, adjacency_all, neighbor_all, counts_all, wanted, cotangent_all, groups))
    loss_scale = NODES ** -0.5
    return grad_features.reshape(NODES, F), sums[0] * loss_scale, sums[1] * loss_scale
```

```python
import math

import jax
import jax.numpy as jnp
from jax import lax
from jax.sharding import PartitionSpec as P

NX, NZ, NC = 4, 8, 2


def place(x, z, c):
    return (x % NX) * (NZ * NC) + (z % NZ) * NC + c


def move(a, dx=0, dz=0, dc=0):
    pairs = [
        (place(x, z, c), place(x + dx, z + dz, c ^ dc))
        for x in range(NX)
        for z in range(NZ)
        for c in range(NC)
    ]
    return lax.ppermute(a, "dom", pairs)


def gather_plane(e0, e1):
    half = e0.shape[0] // 2
    zp1, zm1 = move(e0, dz=1), move(e0, dz=-1)
    xp1, xm1 = move(e1, dx=1), move(e1, dx=-1)
    zp2, zm2 = move(zp1, dz=1), move(zm1, dz=-1)
    x2a, x2b = move(xp1[:half], dx=1), move(xm1[half:], dx=-1)
    j1 = jnp.stack([e1, xp1])
    j2 = jnp.stack([xm1, jnp.concatenate([x2a, x2b])])
    h1 = jnp.stack([e0, zp1, zm1, zp2])
    zp3, zm3 = move(zp2, dz=1), move(zm2, dz=-1)
    z4 = jnp.concatenate([move(zp3[:half], dz=1), move(zm3[half:], dz=-1)])
    h2 = jnp.stack([zm2, zp3, zm3, z4])
    zs = ((0, -1, 1, -2), (2, -3, 3, 4))
    first = {}
    for h, dzs in zip((h1, h2), zs):
        p, m = move(h, dx=1), move(h, dx=-1)
        fp, fm = move(p[:2], dx=1), move(m[2:], dx=-1)
        for i, dz in enumerate(dzs):
            first[0, dz % NZ] = h[i]
            first[3, dz % NZ] = p[i]
            first[1, dz % NZ] = m[i]
            first[2, dz % NZ] = fp[i] if i < 2 else fm[i - 2]
    second = {}
    for j, dxs in ((j1, (0, -1)), (j2, (1, 2))):
        s1p, s1m = move(j, dz=1), move(j, dz=-1)
        s2p, s2m = move(s1p, dz=1), move(s1m, dz=-1)
        s3p, s3m = move(s2p, dz=1), move(s2m, dz=-1)
        s4p, s4m = move(s3p[:1], dz=1), move(s3m[1:], dz=-1)
        for i, dx in enumerate(dxs):
            dx = dx % NX
            second[dx, 0] = j[i]
            second[dx, 7], second[dx, 1] = s1p[i], s1m[i]
            second[dx, 6], second[dx, 2] = s2p[i], s2m[i]
            second[dx, 5], second[dx, 3] = s3p[i], s3m[i]
            second[dx, 4] = s4p[0] if i == 0 else s4m[0]
    return first, second


def local(
    features, boundary_cache, adjacency, neighbor, counts, wanted, weight_in, weight_out, cotangent
):
    nblocks = adjacency.shape[0]
    slot_total = adjacency.shape[1]
    block_rows = adjacency.shape[2]
    channels = features.shape[1]
    node_rows = nblocks * block_rows
    partners = lax.axis_size("dom")
    position = lax.axis_index("dom")
    mx, mz, mc = position // (NZ * NC), position // NC % NZ, position % NC
    cache_copy = boundary_cache.astype(jnp.bfloat16)
    first, second = gather_plane(cache_copy[:block_rows], cache_copy[block_rows:])
    order = [(dx, dz) for dx in range(NX) for dz in range(NZ)]
    first = jnp.stack([first[o] for o in order])
    second = jnp.stack([second[o] for o in order])
    selected = wanted[0].reshape(NX, NZ, NC)
    selected = jnp.roll(selected, (-mx, -mz), (0, 1)).reshape(NX * NZ, NC)
    other = move(wanted[0], dc=1).reshape(NX, NZ, NC)
    other = jnp.roll(other, (-mx, -mz), (0, 1)).reshape(NX * NZ, NC)
    mine = jnp.where(mc == 0, selected[:, 0], selected[:, 1])
    theirs = jnp.where(mc == 0, other[:, 0], other[:, 1])
    given = move(jnp.where((theirs == 1)[:, None, None], second, first), dc=1)
    kept = jnp.where((mine == 1)[:, None, None], second, first)
    owned = features.reshape(nblocks, block_rows, channels)
    sources = jnp.concatenate([owned, kept, given], 0)
    q = neighbor - nblocks
    qx, qz, qc = q // (NZ * NC), q // NC % NZ, q % NC
    rel = (qx - mx) % NX * NZ + (qz - mz) % NZ + jnp.where(qc == mc, 0, NX * NZ)
    slot = jnp.where(neighbor < nblocks, neighbor, nblocks + rel)

    active = jnp.arange(slot_total)[None, :] < counts[:, None]
    chosen = sources[slot]
    chosen = jnp.where(active[:, :, None, None], chosen, jnp.zeros_like(chosen))
    aggregate = jnp.einsum("bsij,bsjf->bif", adjacency, chosen, preferred_element_type=jnp.float32)
    aggregate = aggregate.astype(jnp.bfloat16).reshape(node_rows, channels)
    joined = jnp.concatenate([aggregate, features], 1)
    preact = jnp.dot(joined, weight_in, preferred_element_type=jnp.float32)
    gating = jax.nn.sigmoid(preact)
    hidden = (preact * gating).astype(jnp.bfloat16)
    grad_hidden = jnp.einsum("nf,hf->nh", cotangent, weight_out, preferred_element_type=jnp.float32)
    grad_preact = (grad_hidden * gating * (1.0 + preact * (1.0 - gating))).astype(jnp.bfloat16)
    grad_joined = jnp.einsum(
        "nh,ch->nc", grad_preact, weight_in, preferred_element_type=jnp.float32
    )
    grad_aggregate = (
        grad_joined[:, :channels].astype(jnp.bfloat16).reshape(nblocks, block_rows, channels)
    )
    backward = jnp.einsum(
        "bsji,bjf->bsif", adjacency, grad_aggregate, preferred_element_type=jnp.float32
    )
    local_hit = active & (neighbor < nblocks)
    routing = (neighbor[None, :, :] == jnp.arange(nblocks)[:, None, None]) & local_hit[None]
    spread = jnp.einsum(
        "cbs,bsif->cif", routing.astype(jnp.float32), backward, precision=lax.Precision.HIGHEST
    )
    grad_features = (grad_joined[:, channels:] + spread.reshape(node_rows, channels)).astype(
        jnp.bfloat16
    )
    node_total = node_rows * lax.axis_size("grp") * partners
    loss_scale = 1.0 / math.sqrt(node_total)
    term_in = jnp.einsum("nc,nh->ch", joined, grad_preact, preferred_element_type=jnp.float32)
    term_out = jnp.einsum("nh,nf->hf", hidden, cotangent, preferred_element_type=jnp.float32)
    terms = jnp.concatenate([term_in, term_out], 1) * loss_scale
    total = reduce_terms(terms, mc)
    hid = weight_in.shape[1]
    return (grad_features, total[:, :hid], total[:, hid:])


def reduce_terms(terms, mc):
    width = terms.shape[1]
    terms = terms.reshape(NX * NZ, NC, -1, width)
    keep = jnp.where(mc == 0, terms[:, 0], terms[:, 1])
    send = jnp.where(mc == 0, terms[:, 1], terms[:, 0])
    keep = keep + move(send, dc=1)
    same = [[place(x, z, c) for x in range(NX) for z in range(NZ)] for c in range(NC)]
    keep = lax.all_to_all(keep, "dom", 0, 0, axis_index_groups=same).sum(0)
    flip = lambda k: lax.ppermute(keep, "grp", [(i, i ^ k) for i in range(4)])
    return (keep + flip(1)) + (flip(2) + flip(3))


def solution(mesh):
    in_specs = (
        P(("grp", "dom"), None),
        P(("grp", "dom"), None),
        P(("grp", "dom"), None, None, None),
        P(("grp", "dom"), None),
        P(("grp", "dom")),
        P(("grp", "dom"), None),
        P(),
        P(),
        P(("grp", "dom"), None),
    )
    out_specs = (P(("grp", "dom"), None), P("dom", None), P("dom", None))
    return jax.shard_map(local, mesh=mesh, in_specs=in_specs, out_specs=out_specs, check_vma=False)
```

```python
import math

import jax
import jax.numpy as jnp
from jax import lax
from jax.experimental import pallas as pl
from jax.experimental.pallas import tpu as pltpu
from jax.sharding import PartitionSpec as P

NX, NZ, NC = 4, 8, 2


def place(x, z, c):
    return (x % NX) * (NZ * NC) + (z % NZ) * NC + c


def move(a, dx=0, dz=0, dc=0):
    pairs = [
        (place(x, z, c), place(x + dx, z + dz, c ^ dc))
        for x in range(NX)
        for z in range(NZ)
        for c in range(NC)
    ]
    return lax.ppermute(a, "dom", pairs)


BF = jnp.bfloat16
F32 = jnp.float32


class Table:
    def __init__(self, rows):
        self.rows, self.arrays, self.spots = rows, [], {}

    def add(self, array, places):
        self.arrays.append(array)
        n = len(self.arrays) - 1
        for i, (key, row, rows) in enumerate(places):
            self.spots.setdefault(key, []).append((n, i, row, rows))


def gather_plane(e0, e1):
    rows = e0.shape[1]
    half = rows // 2
    t = Table(rows)

    def whole(a, *keys):
        t.add(a, [((e, dx % NX, dz % NZ), 0, rows) for e, dx, dz in keys])
        return a

    def part(a, key, row):
        e, dx, dz = key
        t.add(a, [((e, dx % NX, dz % NZ), row, half)])
        return a

    zp1, zm1 = move(e0, dz=1), move(e0, dz=-1)
    xp1, xm1 = move(e1, dx=1), move(e1, dx=-1)
    zp2, zm2 = move(zp1, dz=1), move(zm1, dz=-1)
    x2a, x2b = move(xp1[:, :half], dx=1), move(xm1[:, half:], dx=-1)
    j = jnp.concatenate([e1, xp1, xm1, jnp.concatenate([x2a, x2b], 1)])
    zp3, zm3 = move(zp2, dz=1), move(zm2, dz=-1)
    z4a, z4b = move(zp3[:, :half], dz=1), move(zm3[:, half:], dz=-1)
    h = jnp.concatenate([e0, zp1, zm1, zp2, zm2, zp3, zm3, jnp.concatenate([z4a, z4b], 1)])
    zs = (0, -1, 1, -2, 2, -3, 3, 4)
    whole(h, *[(0, 0, z) for z in zs])
    p, m = move(h, dx=1), move(h, dx=-1)
    whole(p, *[(0, -1, z) for z in zs])
    whole(m, *[(0, 1, z) for z in zs])
    whole(move(p[:4], dx=1), *[(0, 2, z) for z in zs[:4]])
    whole(move(m[4:], dx=-1), *[(0, 2, z) for z in zs[4:]])
    xs = (0, -1, 1, 2)
    whole(j, *[(1, x, 0) for x in xs])
    sp, sm = j, j
    for k in (1, 2, 3):
        sp, sm = move(sp, dz=1), move(sm, dz=-1)
        whole(sp, *[(1, x, -k) for x in xs])
        whole(sm, *[(1, x, k) for x in xs])
    whole(move(sp[:2], dz=1), *[(1, x, 4) for x in xs[:2]])
    whole(move(sm[2:], dz=-1), *[(1, x, 4) for x in xs[2:]])
    return t


def pick(table, want, position):
    channels = table.arrays[0].shape[-1]

    def kernel(want_ref, at_ref, *refs):
        pieces, out, sems = refs[:-2], refs[-2], refs[-1]
        mx, mz, mc = at_ref[0], at_ref[1], at_ref[2]

        def copy(i, e, dx, dz):
            return [
                pltpu.make_async_copy(
                    pieces[n].at[k, pl.ds(row, rows)], out.at[i, pl.ds(row, rows)], sems.at[i, s]
                )
                for s, (n, k, row, rows) in enumerate(table.spots[e, dx, dz])
            ]

        for dx in range(NX):
            for dz in range(NZ):
                i = dx * NZ + dz
                q = place_of(mx + dx, mz + dz, mc)
                second = want_ref[0, q] == 1

                @pl.when(second)
                def _():
                    for c in copy(i, 1, dx, dz):
                        c.start()

                @pl.when(jnp.logical_not(second))
                def _():
                    for c in copy(i, 0, dx, dz):
                        c.start()

        for dx in range(NX):
            for dz in range(NZ):
                for c in copy(dx * NZ + dz, 0, dx, dz):
                    c.wait()

    return pl.pallas_call(
        kernel,
        out_shape=jax.ShapeDtypeStruct((NX * NZ, table.rows, channels), BF),
        in_specs=[pl.BlockSpec(memory_space=pltpu.SMEM)] * 2
        + [pl.BlockSpec(memory_space=pl.ANY)] * len(table.arrays),
        out_specs=pl.BlockSpec(memory_space=pl.ANY),
        scratch_shapes=[pltpu.SemaphoreType.DMA((NX * NZ, 1))],
        name="pick",
    )(want, position, *table.arrays)


def place_of(x, z, c):
    x = jnp.where(x >= NX, x - NX, x)
    z = jnp.where(z >= NZ, z - NZ, z)
    return x * (NZ * NC) + z * NC + c


def dot(a, b, ca, cb):
    return lax.dot_general(a, b, (((ca,), (cb,)), ((), ())), preferred_element_type=F32)


def forward(features, kept, given, adjacency, cotangent, weight_in, weight_out, neighbor, counts, position, scale):
    nblocks, slots, rows, _ = adjacency.shape
    nodes, channels = features.shape
    hid = weight_in.shape[1]
    per = 4
    tile = per * rows
    steps = nblocks // per

    def kernel(nb_ref, cnt_ref, at_ref, feat, kept_ref, given_ref, adj, cot, win, wout, gp_out, keep, send, src, joined, acc_in, acc_out):
        step = pl.program_id(0)
        mx, mz, mc = at_ref[0], at_ref[1], at_ref[2]

        @pl.when(step == 0)
        def _():
            acc_in[...] = jnp.zeros_like(acc_in)
            acc_out[...] = jnp.zeros_like(acc_out)

        for j in range(per):
            b = step * per + j
            for s in range(slots):
                nb = nb_ref[b, s]
                live = s < cnt_ref[b]
                q = nb - nblocks
                qx, qz, qc = q >> 4, (q >> 1) & 7, q & 1
                rel = ((qx - mx) & 3) * NZ + ((qz - mz) & 7)
                rel = jnp.where(nb < nblocks, 0, rel)
                same = qc == mc
                dst = src.at[j, pl.ds(s * rows, rows)]

                @pl.when(jnp.logical_and(live, nb < nblocks))
                def _():
                    dst[...] = feat[pl.ds(pl.multiple_of(jnp.minimum(nb, nblocks - 1) * rows, rows), rows), :]

                @pl.when(jnp.logical_and(live, jnp.logical_and(nb >= nblocks, same)))
                def _():
                    dst[...] = kept_ref[rel]

                @pl.when(jnp.logical_and(live, jnp.logical_and(nb >= nblocks, jnp.logical_not(same))))
                def _():
                    dst[...] = given_ref[rel]

                @pl.when(jnp.logical_not(live))
                def _():
                    dst[...] = jnp.zeros((rows, channels), BF)

        for j in range(per):
            agg = dot(adj[j, 0], src[j, :rows], 1, 0)
            for s in range(1, slots):
                agg += dot(adj[j, s], src[j, s * rows : (s + 1) * rows], 1, 0)
            joined[j * rows : (j + 1) * rows, :channels] = agg.astype(BF)
        joined[:, channels:] = feat[pl.ds(pl.multiple_of(step * tile, tile), tile), :]
        x = joined[...]
        g = cot[...]
        pre = dot(x, win[...], 1, 0)
        gh = dot(g, wout[...], 1, 1)
        sg = jax.nn.sigmoid(pre)
        hidden = (pre * sg).astype(BF)
        gp = (gh * sg * (1.0 + pre * (1.0 - sg))).astype(BF)
        gp_out[...] = gp
        acc_in[...] += dot(x, gp, 0, 0)
        acc_out[...] += dot(hidden, g, 0, 0)

        @pl.when(step == steps - 1)
        def _():
            for i in range(NX * NZ):
                for ref, c in ((keep, mc), (send, 1 - mc)):
                    at = pl.multiple_of((2 * i + c) * 8, 8)
                    ref[i, :, :hid] = acc_in[pl.ds(at, 8), :] * scale
                    ref[i, :, hid:] = acc_out[pl.ds(at, 8), :] * scale

    smem = pl.BlockSpec(memory_space=pltpu.SMEM)
    full = lambda a: pl.BlockSpec(a.shape, lambda i: (0,) * a.ndim, pipeline_mode=pl.Buffered(1))
    part = (NX * NZ, 8, hid + channels)
    return pl.pallas_call(
        kernel,
        grid=(steps,),
        out_shape=[
            jax.ShapeDtypeStruct((nodes, hid), BF),
            jax.ShapeDtypeStruct(part, F32),
            jax.ShapeDtypeStruct(part, F32),
        ],
        in_specs=[smem, smem, smem, full(features), full(kept), full(given)]
        + [
            pl.BlockSpec((per, slots, rows, rows), lambda i: (i, 0, 0, 0)),
            pl.BlockSpec((tile, channels), lambda i: (i, 0)),
            full(weight_in),
            full(weight_out),
        ],
        out_specs=[
            pl.BlockSpec((tile, hid), lambda i: (i, 0)),
            pl.BlockSpec(part, lambda i: (0, 0, 0)),
            pl.BlockSpec(part, lambda i: (0, 0, 0)),
        ],
        scratch_shapes=[
            pltpu.VMEM((per, slots * rows, channels), BF),
            pltpu.VMEM((tile, 2 * channels), BF),
            pltpu.VMEM((2 * channels, hid), F32),
            pltpu.VMEM((hid, channels), F32),
        ],
        name="forward",
        compiler_params=pltpu.CompilerParams(vmem_limit_bytes=48 << 20),
    )(neighbor, counts, position, features, kept, given, adjacency, cotangent, weight_in, weight_out)


def backward(grad_preact, weight_in, adjacency, neighbor, counts):
    nblocks, slots, rows, _ = adjacency.shape
    nodes, hid = grad_preact.shape
    channels = weight_in.shape[0] // 2
    per = 4
    tile = per * rows
    steps = nblocks // per

    def kernel(nb_ref, cnt_ref, gp, win, adj, out, acc):
        step = pl.program_id(0)

        @pl.when(step == 0)
        def _():
            acc[...] = jnp.zeros_like(acc)

        gj = dot(gp[...], win[...], 1, 1)
        mine = pl.ds(pl.multiple_of(step * tile, tile), tile)
        acc[mine, :] = acc[mine, :] + gj[:, channels:]
        ga = gj[:, :channels].astype(BF)
        for j in range(per):
            b = step * per + j
            for s in range(slots):
                nb = nb_ref[b, s]

                @pl.when(jnp.logical_and(s < cnt_ref[b], nb < nblocks))
                def _():
                    at = pl.ds(pl.multiple_of(jnp.minimum(nb, nblocks - 1) * rows, rows), rows)
                    acc[at, :] = acc[at, :] + dot(adj[j, s], ga[j * rows : (j + 1) * rows], 0, 0)

        @pl.when(step == steps - 1)
        def _():
            out[...] = acc[...].astype(BF)

    smem = pl.BlockSpec(memory_space=pltpu.SMEM)
    return pl.pallas_call(
        kernel,
        grid=(steps,),
        out_shape=jax.ShapeDtypeStruct((nodes, channels), BF),
        in_specs=[
            smem,
            smem,
            pl.BlockSpec((tile, hid), lambda i: (i, 0)),
            pl.BlockSpec(weight_in.shape, lambda i: (0, 0), pipeline_mode=pl.Buffered(1)),
            pl.BlockSpec((per, slots, rows, rows), lambda i: (i, 0, 0, 0)),
        ],
        out_specs=pl.BlockSpec((nodes, channels), lambda i: (0, 0)),
        scratch_shapes=[pltpu.VMEM((nodes, channels), F32)],
        name="backward",
        cost_estimate=pl.CostEstimate(
            flops=2 * nodes * (2 * hid * channels + slots * rows * channels),
            bytes_accessed=2 * nodes * (hid + 3 * channels),
            transcendentals=0,
        ),
        compiler_params=pltpu.CompilerParams(vmem_limit_bytes=32 << 20),
    )(neighbor, counts, grad_preact, weight_in, adjacency)


def local(
    features, boundary_cache, adjacency, neighbor, counts, wanted, weight_in, weight_out, cotangent
):
    block_rows = adjacency.shape[2]
    channels = features.shape[1]
    hid = weight_in.shape[1]
    at = lax.axis_index("dom")
    position = jnp.stack([at // (NZ * NC), at // NC % NZ, at % NC]).astype(jnp.int32)
    exported = boundary_cache.astype(BF).reshape(-1, block_rows, channels)
    table = gather_plane(exported[:1], exported[1:])
    given = move(pick(table, move(wanted, dc=1), position), dc=1)
    kept = pick(table, wanted, position)
    node_total = features.shape[0] * lax.axis_size("grp") * lax.axis_size("dom")
    scale = 1.0 / math.sqrt(node_total)
    grad_preact, keep, send = forward(
        features, kept, given, adjacency, cotangent, weight_in, weight_out, neighbor, counts, position, scale
    )
    keep = keep + move(send, dc=1)
    same = [[place(x, z, c) for x in range(NX) for z in range(NZ)] for c in range(NC)]
    keep = lax.all_to_all(keep, "dom", 0, 0, axis_index_groups=same).sum(0)
    grad_features = backward(grad_preact, weight_in, adjacency, neighbor, counts)
    flip = lambda k: lax.ppermute(keep, "grp", [(i, i ^ k) for i in range(4)])
    total = (keep + flip(1)) + (flip(2) + flip(3))
    return (grad_features, total[:, :hid], total[:, hid:])


def solution(mesh):
    in_specs = (
        P(("grp", "dom"), None),
        P(("grp", "dom"), None),
        P(("grp", "dom"), None, None, None),
        P(("grp", "dom"), None),
        P(("grp", "dom")),
        P(("grp", "dom"), None),
        P(),
        P(),
        P(("grp", "dom"), None),
    )
    out_specs = (P(("grp", "dom"), None), P("dom", None), P("dom", None))
    return jax.shard_map(local, mesh=mesh, in_specs=in_specs, out_specs=out_specs, check_vma=False)
```

```python
import math

import jax
import jax.numpy as jnp
from jax import lax
from jax.experimental import pallas as pl
from jax.experimental.pallas import tpu as pltpu
from jax.sharding import PartitionSpec as P

NX, NZ, NC = 4, 8, 2


def place(x, z, c):
    return (x % NX) * (NZ * NC) + (z % NZ) * NC + c


def move(a, dx=0, dz=0, dc=0):
    pairs = [
        (place(x, z, c), place(x + dx, z + dz, c ^ dc))
        for x in range(NX)
        for z in range(NZ)
        for c in range(NC)
    ]
    return lax.ppermute(a, "dom", pairs)


BF = jnp.bfloat16
F32 = jnp.float32


class Table:
    def __init__(self):
        self.arrays, self.spots = [], {}

    def add(self, array, xs, dz):
        self.arrays.append(array)
        for i, dx in enumerate(xs):
            for e in range(2):
                self.spots[e, dx % NX, dz % NZ] = (len(self.arrays) - 1, 2 * i + e)


def gather_plane(own):
    t = Table()
    c1, c2, c3 = move(own, dx=1), move(own, dx=-1), move(own, dx=2)
    chunks = [(jnp.concatenate([own, c1]), (0, -1)), (jnp.concatenate([c2, c3]), (1, 2))]
    state = []
    for a, xs in chunks:
        t.add(a, xs, 0)
        state.append((a, a))
    for k in (1, 2, 3):
        for i, (_, xs) in enumerate(chunks):
            p, m = state[i]
            p, m = move(p, dz=1), move(m, dz=-1)
            t.add(p, xs, -k)
            t.add(m, xs, k)
            state[i] = (p, m)
    for i, (_, xs) in enumerate(chunks):
        p, m = state[i]
        t.add(move(p[:2], dz=1), xs[:1], 4)
        t.add(move(m[2:], dz=-1), xs[1:], 4)
    return t


def pick(table, want, position):
    block = table.arrays[0].shape[1:]

    def kernel(want_ref, at_ref, *refs):
        pieces, out, sems = refs[:-2], refs[-2], refs[-1]
        mx, mz, mc = at_ref[0], at_ref[1], at_ref[2]

        def copy(e, dx, dz):
            n, k = table.spots[e, dx, dz]
            i = dx * NZ + dz
            return pltpu.make_async_copy(pieces[n].at[k], out.at[i], sems.at[i])

        spots = [(dx, dz) for dx in range(NX) for dz in range(NZ)]
        for dx, dz in spots:
            second = want_ref[0, place_of(mx + dx, mz + dz, mc)] == 1
            for e in range(2):

                @pl.when(second if e else jnp.logical_not(second))
                def _():
                    copy(e, dx, dz).start()

        for dx, dz in spots:
            copy(0, dx, dz).wait()

    return pl.pallas_call(
        kernel,
        out_shape=jax.ShapeDtypeStruct((NX * NZ, *block), BF),
        in_specs=[pl.BlockSpec(memory_space=pltpu.SMEM)] * 2
        + [pl.BlockSpec(memory_space=pl.ANY)] * len(table.arrays),
        out_specs=pl.BlockSpec(memory_space=pltpu.VMEM),
        scratch_shapes=[pltpu.SemaphoreType.DMA((NX * NZ,))],
        name="pick",
    )(want, position, *table.arrays)


def place_of(x, z, c):
    x = jnp.where(x >= NX, x - NX, x)
    z = jnp.where(z >= NZ, z - NZ, z)
    return x * (NZ * NC) + z * NC + c


def dot(a, b, ca, cb):
    return lax.dot_general(a, b, (((ca,), (cb,)), ((), ())), preferred_element_type=F32)


def forward(features, kept, given, adjacency, cotangent, weight_in, weight_out, neighbor, counts, position, scale):
    nblocks, slots, rows, _ = adjacency.shape
    nodes, channels = features.shape
    hid = weight_in.shape[1]
    per = 4
    tile = per * rows
    steps = nblocks // per

    def kernel(nb_ref, cnt_ref, at_ref, feat, kept_ref, given_ref, adj, cot, win, wout, gp_out, keep, send, src, joined, acc_in, acc_out):
        step = pl.program_id(0)
        mx, mz, mc = at_ref[0], at_ref[1], at_ref[2]

        @pl.when(step == 0)
        def _():
            acc_in[...] = jnp.zeros_like(acc_in)
            acc_out[...] = jnp.zeros_like(acc_out)

        for j in range(per):
            b = step * per + j
            for s in range(slots):
                nb = nb_ref[b, s]
                live = s < cnt_ref[b]
                q = nb - nblocks
                qx, qz, qc = q >> 4, (q >> 1) & 7, q & 1
                rel = ((qx - mx) & 3) * NZ + ((qz - mz) & 7)
                rel = jnp.where(nb < nblocks, 0, rel)
                same = qc == mc
                dst = src.at[j, pl.ds(s * rows, rows)]

                @pl.when(jnp.logical_and(live, nb < nblocks))
                def _():
                    dst[...] = feat[pl.ds(pl.multiple_of(jnp.minimum(nb, nblocks - 1) * rows, rows), rows), :]

                @pl.when(jnp.logical_and(live, jnp.logical_and(nb >= nblocks, same)))
                def _():
                    dst[...] = kept_ref[rel]

                @pl.when(jnp.logical_and(live, jnp.logical_and(nb >= nblocks, jnp.logical_not(same))))
                def _():
                    dst[...] = given_ref[rel]

                @pl.when(jnp.logical_not(live))
                def _():
                    dst[...] = jnp.zeros((rows, channels), BF)

        for j in range(per):
            agg = dot(adj[j, 0], src[j, :rows], 1, 0)
            for s in range(1, slots):
                agg += dot(adj[j, s], src[j, s * rows : (s + 1) * rows], 1, 0)
            joined[j * rows : (j + 1) * rows, :channels] = agg.astype(BF)
        joined[:, channels:] = feat[pl.ds(pl.multiple_of(step * tile, tile), tile), :]
        x = joined[...]
        g = cot[...]
        pre = dot(x, win[...], 1, 0)
        gh = dot(g, wout[...], 1, 1)
        sg = jax.nn.sigmoid(pre)
        hidden = (pre * sg).astype(BF)
        gp = (gh * sg * (1.0 + pre * (1.0 - sg))).astype(BF)
        gp_out[...] = gp
        acc_in[...] += dot(x, gp, 0, 0)
        acc_out[...] += dot(hidden, g, 0, 0)

        @pl.when(step == steps - 1)
        def _():
            for i in range(NX * NZ):
                for ref, c in ((keep, mc), (send, 1 - mc)):
                    at = pl.multiple_of((2 * i + c) * 8, 8)
                    ref[i, :, :hid] = acc_in[pl.ds(at, 8), :] * scale
                    ref[i, :, hid:] = acc_out[pl.ds(at, 8), :] * scale

    smem = pl.BlockSpec(memory_space=pltpu.SMEM)
    full = lambda a: pl.BlockSpec(memory_space=pltpu.VMEM)
    part = (NX * NZ, 8, hid + channels)
    return pl.pallas_call(
        kernel,
        grid=(steps,),
        out_shape=[
            jax.ShapeDtypeStruct((nodes, hid), BF),
            jax.ShapeDtypeStruct(part, F32),
            jax.ShapeDtypeStruct(part, F32),
        ],
        in_specs=[smem, smem, smem, full(features), full(kept), full(given)]
        + [
            pl.BlockSpec((per, slots, rows, rows), lambda i: (i, 0, 0, 0)),
            pl.BlockSpec((tile, channels), lambda i: (i, 0)),
            full(weight_in),
            full(weight_out),
        ],
        out_specs=[
            pl.BlockSpec((tile, hid), lambda i: (i, 0)),
            pl.BlockSpec(part, lambda i: (0, 0, 0)),
            pl.BlockSpec(part, lambda i: (0, 0, 0)),
        ],
        scratch_shapes=[
            pltpu.VMEM((per, slots * rows, channels), BF),
            pltpu.VMEM((tile, 2 * channels), BF),
            pltpu.VMEM((2 * channels, hid), F32),
            pltpu.VMEM((hid, channels), F32),
        ],
        name="forward",
        compiler_params=pltpu.CompilerParams(vmem_limit_bytes=48 << 20),
    )(neighbor, counts, position, features, kept, given, adjacency, cotangent, weight_in, weight_out)


def backward(grad_preact, weight_in, adjacency, neighbor, counts):
    nblocks, slots, rows, _ = adjacency.shape
    nodes, hid = grad_preact.shape
    channels = weight_in.shape[0] // 2
    per = 4
    tile = per * rows
    steps = nblocks // per

    def kernel(nb_ref, cnt_ref, gp, win, adj, out, acc):
        step = pl.program_id(0)

        @pl.when(step == 0)
        def _():
            acc[...] = jnp.zeros_like(acc)

        gj = dot(gp[...], win[...], 1, 1)
        mine = pl.ds(pl.multiple_of(step * tile, tile), tile)
        acc[mine, :] = acc[mine, :] + gj[:, channels:]
        ga = gj[:, :channels].astype(BF)
        for j in range(per):
            b = step * per + j
            for s in range(slots):
                nb = nb_ref[b, s]

                @pl.when(jnp.logical_and(s < cnt_ref[b], nb < nblocks))
                def _():
                    at = pl.ds(pl.multiple_of(jnp.minimum(nb, nblocks - 1) * rows, rows), rows)
                    acc[at, :] = acc[at, :] + dot(adj[j, s], ga[j * rows : (j + 1) * rows], 0, 0)

        @pl.when(step == steps - 1)
        def _():
            out[...] = acc[...].astype(BF)

    smem = pl.BlockSpec(memory_space=pltpu.SMEM)
    return pl.pallas_call(
        kernel,
        grid=(steps,),
        out_shape=jax.ShapeDtypeStruct((nodes, channels), BF),
        in_specs=[
            smem,
            smem,
            pl.BlockSpec((tile, hid), lambda i: (i, 0)),
            pl.BlockSpec(weight_in.shape, lambda i: (0, 0), pipeline_mode=pl.Buffered(1)),
            pl.BlockSpec((per, slots, rows, rows), lambda i: (i, 0, 0, 0)),
        ],
        out_specs=pl.BlockSpec((nodes, channels), lambda i: (0, 0)),
        scratch_shapes=[pltpu.VMEM((nodes, channels), F32)],
        name="backward",
        cost_estimate=pl.CostEstimate(
            flops=2 * nodes * (2 * hid * channels + slots * rows * channels),
            bytes_accessed=2 * nodes * (hid + 3 * channels),
            transcendentals=0,
        ),
        compiler_params=pltpu.CompilerParams(vmem_limit_bytes=32 << 20),
    )(neighbor, counts, grad_preact, weight_in, adjacency)


def local(
    features, boundary_cache, adjacency, neighbor, counts, wanted, weight_in, weight_out, cotangent
):
    block_rows = adjacency.shape[2]
    channels = features.shape[1]
    hid = weight_in.shape[1]
    at = lax.axis_index("dom")
    position = jnp.stack([at // (NZ * NC), at // NC % NZ, at % NC]).astype(jnp.int32)
    exported = boundary_cache.astype(BF).reshape(-1, block_rows, channels)
    other = move(wanted, dc=1)
    table = gather_plane(exported)
    given = move(pick(table, other, position), dc=1)
    kept = pick(table, wanted, position)
    node_total = features.shape[0] * lax.axis_size("grp") * lax.axis_size("dom")
    scale = 1.0 / math.sqrt(node_total)
    grad_preact, keep, send = forward(
        features, kept, given, adjacency, cotangent, weight_in, weight_out, neighbor, counts, position, scale
    )
    keep = keep + move(send, dc=1)
    same = [[place(x, z, c) for x in range(NX) for z in range(NZ)] for c in range(NC)]
    keep = lax.all_to_all(keep, "dom", 0, 0, axis_index_groups=same).sum(0)
    grad_features = backward(grad_preact, weight_in, adjacency, neighbor, counts)
    flip = lambda k: lax.ppermute(keep, "grp", [(i, i ^ k) for i in range(4)])
    total = (keep + flip(1)) + (flip(2) + flip(3))
    return (grad_features, total[:, :hid], total[:, hid:])


def solution(mesh):
    in_specs = (
        P(("grp", "dom"), None),
        P(("grp", "dom"), None),
        P(("grp", "dom"), None, None, None),
        P(("grp", "dom"), None),
        P(("grp", "dom")),
        P(("grp", "dom"), None),
        P(),
        P(),
        P(("grp", "dom"), None),
    )
    out_specs = (P(("grp", "dom"), None), P("dom", None), P("dom", None))
    return jax.shard_map(local, mesh=mesh, in_specs=in_specs, out_specs=out_specs, check_vma=False)
```

```python
import math

import jax
import jax.numpy as jnp
from jax import lax
from jax.experimental import pallas as pl
from jax.experimental.pallas import tpu as pltpu
from jax.sharding import PartitionSpec as P


NX, NZ, NC = 4, 8, 2


def place(x, z, c):
    return (x % NX) * (NZ * NC) + (z % NZ) * NC + c


def move(a, dx=0, dz=0, dc=0):
    pairs = [
        (place(x, z, c), place(x + dx, z + dz, c ^ dc))
        for x in range(NX)
        for z in range(NZ)
        for c in range(NC)
    ]
    return lax.ppermute(a, "dom", pairs)


BF = jnp.bfloat16
F32 = jnp.float32
WIRE = jnp.bfloat16
PER = 6


class Table:
    def __init__(self):
        self.arrays, self.spots = [], {}

    def add(self, array, xs, dz):
        self.arrays.append(array)
        for i, dx in enumerate(xs):
            self.spots[dx % NX, dz % NZ] = (len(self.arrays) - 1, 2 * i)


def gather_plane(own):
    near = Table()

    def go(a, **step):
        return move(a, **step)

    c1, c2, c3 = go(own, dx=1), go(own, dx=-1), go(own, dx=2)
    p, q = jnp.concatenate([own, c2]), jnp.concatenate([c1, c3])
    px, qx = (0, 1), (-1, 2)
    near.add(p, px, 0)
    near.add(q, qx, 0)
    pp, pm, qp, qm = p, p, q, q
    for k in (1, 2, 3):
        pp, pm = go(pp, dz=1), go(pm, dz=-1)
        qp, qm = go(qp, dz=1), go(qm, dz=-1)
        near.add(pp, px, -k)
        near.add(pm, px, k)
        near.add(qp, qx, -k)
        near.add(qm, qx, k)
    p4 = go(pp, dz=1)
    given_p = move(p4, dc=1)
    q4 = go(qm, dz=-1)
    given_q = move(q4, dc=1)
    return near, (p4, q4, given_p, given_q)


def pick(table, wants, position):
    block = table.arrays[0].shape[1:]
    spots = sorted(table.spots)
    count, sides = len(spots), len(wants)

    def kernel(*refs):
        want_refs, at_ref, pieces = refs[:sides], refs[sides], refs[sides + 1 : -sides - 2]
        outs, buf, sems = refs[-sides - 2 : -2], refs[-2], refs[-1]
        mx, mz, mc = at_ref[0], at_ref[1], at_ref[2]

        def take(o, i, e):
            n, k = table.spots[spots[i]]
            return pltpu.make_async_copy(pieces[n].at[k + e], buf.at[o, i], sems.at[0, o, i])

        def put(o, i):
            return pltpu.make_async_copy(buf.at[o, i], outs[o].at[i], sems.at[1, o, i])

        every = [(o, i) for o in range(sides) for i in range(count)]
        for o, i in every:
            dx, dz = spots[i]
            take(o, i, want_refs[o][0, place_of(mx + dx, mz + dz, mc)]).start()

        for o, i in every:
            take(o, i, 0).wait()
            put(o, i).start()
        for o, i in every:
            put(o, i).wait()

    return pl.pallas_call(
        kernel,
        out_shape=[jax.ShapeDtypeStruct((count, *block), BF)] * sides,
        in_specs=[pl.BlockSpec(memory_space=pltpu.SMEM)] * (sides + 1)
        + [pl.BlockSpec(memory_space=pl.ANY)] * len(table.arrays),
        out_specs=[pl.BlockSpec(memory_space=pl.ANY)] * sides,
        scratch_shapes=[pltpu.VMEM((sides, count, *block), BF), pltpu.SemaphoreType.DMA((2, sides, count))],
        name="pick",
    )(*wants, position, *table.arrays)


def place_of(x, z, c):
    x = jnp.where(x >= NX, x - NX, x)
    z = jnp.where(z >= NZ, z - NZ, z)
    return x * (NZ * NC) + z * NC + c


def dot(a, b, ca, cb):
    return lax.dot_general(a, b, (((ca,), (cb,)), ((), ())), preferred_element_type=F32)


def forward(features, blocks, adjacency, cotangent, weight_in, weight_out, neighbor, counts, wanted, position, scale):
    nblocks, slots, rows, _ = adjacency.shape
    nodes, channels = features.shape
    hid = weight_in.shape[1]
    per = PER
    tile = per * rows
    steps = nblocks // per

    def kernel(
        nb_ref, cnt_ref, want_ref, at_ref, owned, kept, given, p4, q4, given_p, given_q, adj, feat, cot, win, wout,
        gp_out, keep, send, src, joined, acc_in, acc_out, sems,
    ):
        step = pl.program_id(0)
        mx, mz, mc = at_ref[0], at_ref[1], at_ref[2]

        def slot(b, s):
            return src.at[b, pl.ds(s * rows, rows)]

        def fetch(b, s):
            nb = nb_ref[b, s]
            live = s < cnt_ref[b]
            local = nb < nblocks
            q = jnp.maximum(nb - nblocks, 0)
            qx, qz, qc = q >> 4, (q >> 1) & 7, q & 1
            dx, dz = (qx - mx) & 3, (qz - mz) & 7
            far = dz == 4
            rel = dx * 7 + jnp.where(dz > 4, dz - 1, jnp.minimum(dz, 3))
            e = want_ref[0, q]

            def start(ref):
                pltpu.make_async_copy(ref, slot(b, s), sems.at[b, s]).start()

            def start_from(table, tp, tq):
                @pl.when(jnp.logical_not(far))
                def _():
                    start(table.at[rel])

                @pl.when(far)
                def _():
                    @pl.when(dx < 2)
                    def _():
                        start(tp.at[2 * dx + e])

                    @pl.when(dx >= 2)
                    def _():
                        start(tq.at[2 * (3 - dx) + e])

            @pl.when(live)
            def _():
                @pl.when(local)
                def _():
                    start(owned.at[pl.ds(pl.multiple_of(jnp.minimum(nb, nblocks - 1) * rows, rows), rows)])

                @pl.when(jnp.logical_not(local))
                def _():
                    @pl.when(qc == mc)
                    def _():
                        start_from(kept, p4, q4)

                    @pl.when(qc != mc)
                    def _():
                        start_from(given, given_p, given_q)

            @pl.when(jnp.logical_not(live))
            def _():
                src[b, pl.ds(s * rows, rows)] = jnp.zeros((rows, channels), BF)

        @pl.when(step == 0)
        def _():
            @pl.loop(0, nblocks)
            def _(b):
                for s in range(slots):
                    fetch(b, s)

            acc_in[...] = jnp.zeros_like(acc_in)
            acc_out[...] = jnp.zeros_like(acc_out)

        for j in range(per):
            b = step * per + j
            for s in range(slots):

                @pl.when(s < cnt_ref[b])
                def _():
                    pltpu.make_async_copy(owned.at[pl.ds(0, rows)], slot(b, s), sems.at[b, s]).wait()

        for j in range(per):
            b = step * per + j
            agg = dot(adj[j, 0], src[b, :rows], 1, 0)
            for s in range(1, slots):
                agg += dot(adj[j, s], src[b, s * rows : (s + 1) * rows], 1, 0)
            joined[j * rows : (j + 1) * rows, :channels] = agg.astype(BF)
        joined[:, channels:] = feat[...]
        x = joined[...]
        g = cot[...]
        pre = dot(x, win[...], 1, 0)
        gh = dot(g, wout[...], 1, 1)
        sg = 0.5 * jnp.tanh(0.5 * pre) + 0.5
        silu = pre * sg
        hidden = silu.astype(BF)
        gp = (gh * (sg + silu * (1.0 - sg))).astype(BF)
        gp_out[...] = gp
        acc_in[...] += dot(x, gp, 0, 0)
        acc_out[...] += dot(hidden, g, 0, 0)

        @pl.when(step == steps - 1)
        def _():
            for i in range(NX * NZ):
                for ref, c in ((keep, mc), (send, 1 - mc)):
                    x = (i // NZ + mx) & 3
                    at = pl.multiple_of(((x * NZ + i % NZ) * NC + c) * 8, 8)
                    ref[i, :, :hid] = acc_in[pl.ds(at, 8), :] * scale
                    ref[i, :, hid:] = acc_out[pl.ds(at, 8), :] * scale

    smem = pl.BlockSpec(memory_space=pltpu.SMEM)
    whole = pl.BlockSpec(memory_space=pl.ANY)
    fixed = lambda a: pl.BlockSpec(a.shape, lambda i: (0,) * a.ndim, pipeline_mode=pl.Buffered(1))
    tiled = pl.BlockSpec((tile, channels), lambda i: (i, 0))
    part = (NX * NZ, 8, hid + channels)
    return pl.pallas_call(
        kernel,
        grid=(steps,),
        out_shape=[
            jax.ShapeDtypeStruct((nodes, hid), BF),
            jax.ShapeDtypeStruct(part, F32),
            jax.ShapeDtypeStruct(part, F32),
        ],
        in_specs=[smem] * 4
        + [whole] * 7
        + [pl.BlockSpec((per, slots, rows, rows), lambda i: (i, 0, 0, 0)), tiled, tiled, fixed(weight_in), fixed(weight_out)],
        out_specs=[
            pl.BlockSpec((tile, hid), lambda i: (i, 0)),
            pl.BlockSpec(part, lambda i: (0, 0, 0)),
            pl.BlockSpec(part, lambda i: (0, 0, 0)),
        ],
        scratch_shapes=[
            pltpu.VMEM((nblocks, slots * rows, channels), BF),
            pltpu.VMEM((tile, 2 * channels), BF),
            pltpu.VMEM((2 * channels, hid), F32),
            pltpu.VMEM((hid, channels), F32),
            pltpu.SemaphoreType.DMA((nblocks, slots)),
        ],
        name="forward",
    )(neighbor, counts, wanted, position, features, *blocks, adjacency, features, cotangent, weight_in, weight_out)


def backward(grad_preact, weight_in, adjacency, neighbor, counts):
    nblocks, slots, rows, _ = adjacency.shape
    nodes, hid = grad_preact.shape
    channels = weight_in.shape[0] // 2
    per = 4
    tile = per * rows
    steps = nblocks // per

    def kernel(nb_ref, cnt_ref, gp, win, adj, out, acc):
        step = pl.program_id(0)

        @pl.when(step == 0)
        def _():
            acc[...] = jnp.zeros_like(acc)

        gj = dot(gp[...], win[...], 1, 1)
        mine = pl.ds(pl.multiple_of(step * tile, tile), tile)
        acc[mine, :] = acc[mine, :] + gj[:, channels:]
        ga = gj[:, :channels].astype(BF)
        for j in range(per):
            b = step * per + j
            for s in range(slots):
                nb = nb_ref[b, s]

                @pl.when(jnp.logical_and(s < cnt_ref[b], nb < nblocks))
                def _():
                    at = pl.ds(pl.multiple_of(jnp.minimum(nb, nblocks - 1) * rows, rows), rows)
                    acc[at, :] = acc[at, :] + dot(adj[j, s], ga[j * rows : (j + 1) * rows], 0, 0)

        @pl.when(step == steps - 1)
        def _():
            out[...] = acc[...].astype(BF)

    smem = pl.BlockSpec(memory_space=pltpu.SMEM)
    return pl.pallas_call(
        kernel,
        grid=(steps,),
        out_shape=jax.ShapeDtypeStruct((nodes, channels), BF),
        in_specs=[
            smem,
            smem,
            pl.BlockSpec((tile, hid), lambda i: (i, 0)),
            pl.BlockSpec(weight_in.shape, lambda i: (0, 0), pipeline_mode=pl.Buffered(1)),
            pl.BlockSpec((per, slots, rows, rows), lambda i: (i, 0, 0, 0)),
        ],
        out_specs=pl.BlockSpec((nodes, channels), lambda i: (0, 0)),
        scratch_shapes=[pltpu.VMEM((nodes, channels), F32)],
        name="backward",
        cost_estimate=pl.CostEstimate(
            flops=2 * nodes * (2 * hid * channels + slots * rows * channels),
            bytes_accessed=2 * nodes * (hid + 3 * channels),
            transcendentals=0,
        ),
    )(neighbor, counts, grad_preact, weight_in, adjacency)


def reduce_terms(keep, send, hid):
    keep = (keep + move(send, dc=1)).reshape(NX, NZ, *keep.shape[1:])
    there = keep[1:].astype(WIRE)
    parts = []
    for k in (1, 3, 2):
        parts.append(move(there[k - 1], dx=k))
    keep = (keep[0] + parts[0].astype(F32) + parts[1].astype(F32) + parts[2].astype(F32)).astype(WIRE)
    columns = [[place(x, z, c) for z in range(NZ)] for x in range(NX) for c in range(NC)]
    keep = lax.all_to_all(keep, "dom", 0, 0, axis_index_groups=columns).astype(F32).sum(0)
    a, b, c = (lax.ppermute(keep, "grp", [(i, i ^ k) for i in range(4)]) for k in (1, 2, 3))
    at = slice(0, hid), slice(hid, None)
    return [(keep[:, i] + a[:, i]) + (b[:, i] + c[:, i]) for i in at]


def layer(
    features, boundary_cache, adjacency, neighbor, counts, wanted, weight_in, weight_out, cotangent
):
    block_rows = adjacency.shape[2]
    channels = features.shape[1]
    hid = weight_in.shape[1]
    at = lax.axis_index("dom")
    position = jnp.stack([at // (NZ * NC), at // NC % NZ, at % NC]).astype(jnp.int32)
    exported = boundary_cache.astype(BF).reshape(-1, block_rows, channels)
    other = move(wanted, dc=1)
    near, far = gather_plane(exported)
    (given,) = pick(near, (other,), position)
    given = move(given, dc=1)
    (kept,) = pick(near, (wanted,), position)
    node_total = features.shape[0] * lax.axis_size("grp") * lax.axis_size("dom")
    scale = 1.0 / math.sqrt(node_total)
    grad_preact, keep, send = forward(
        features, (kept, given, *far), adjacency, cotangent, weight_in, weight_out,
        neighbor, counts, wanted, position, scale,
    )
    grad_features = backward(grad_preact, weight_in, adjacency, neighbor, counts)
    total = reduce_terms(keep, send, hid)
    return (grad_features, *total)


def solution(mesh):
    in_specs = (
        P(("grp", "dom"), None),
        P(("grp", "dom"), None),
        P(("grp", "dom"), None, None, None),
        P(("grp", "dom"), None),
        P(("grp", "dom")),
        P(("grp", "dom"), None),
        P(),
        P(),
        P(("grp", "dom"), None),
    )
    out_specs = (P(("grp", "dom"), None), P("dom", None), P("dom", None))
    return jax.shard_map(layer, mesh=mesh, in_specs=in_specs, out_specs=out_specs, check_vma=False)
```

```python
import math

import jax
import jax.numpy as jnp
from jax import lax
from jax.experimental import pallas as pl
from jax.experimental.pallas import tpu as pltpu
from jax.sharding import PartitionSpec as P


NX, NZ, NC = 4, 8, 2


def place(x, z, c):
    return (x % NX) * (NZ * NC) + (z % NZ) * NC + c


def move(a, dx=0, dz=0, dc=0):
    pairs = [
        (place(x, z, c), place(x + dx, z + dz, c ^ dc))
        for x in range(NX)
        for z in range(NZ)
        for c in range(NC)
    ]
    return lax.ppermute(a, "dom", pairs)


BF = jnp.bfloat16
F32 = jnp.float32
WIRE = jnp.bfloat16
PER = 6


class Table:
    def __init__(self):
        self.arrays, self.spots = [], {}

    def add(self, array, xs, dz):
        self.arrays.append(array)
        for i, dx in enumerate(xs):
            self.spots[dx % NX, dz % NZ] = (len(self.arrays) - 1, 2 * i)


def gather_plane(own):
    near, first, third = Table(), Table(), Table()

    def go(a, **step):
        return move(a, **step)

    c1, c2, c3 = go(own, dx=1), go(own, dx=-1), go(own, dx=2)
    p, q = jnp.concatenate([own, c2]), jnp.concatenate([c1, c3])
    px, qx = (0, 1), (-1, 2)
    for a, xs in ((p, px), (q, qx)):
        near.add(a, xs, 0)
        first.add(a, xs, 0)
    pp, pm, qp, qm = p, p, q, q
    for k in (1, 2, 3):
        pp, pm = go(pp, dz=1), go(pm, dz=-1)
        qp, qm = go(qp, dz=1), go(qm, dz=-1)
        for a, xs, dz in ((pp, px, -k), (pm, px, k), (qp, qx, -k), (qm, qx, k)):
            near.add(a, xs, dz)
            (first if k < 3 else third).add(a, xs, dz)
    p4 = go(pp, dz=1)
    given_p = move(p4, dc=1)
    q4 = go(qm, dz=-1)
    given_q = move(q4, dc=1)
    return near, first, third, (p4, q4, given_p, given_q)


def pick(table, wants, position):
    block = table.arrays[0].shape[1:]
    spots = sorted(table.spots)
    count, sides = len(spots), len(wants)

    def kernel(*refs):
        want_refs, at_ref, pieces = refs[:sides], refs[sides], refs[sides + 1 : -sides - 2]
        outs, buf, sems = refs[-sides - 2 : -2], refs[-2], refs[-1]
        mx, mz, mc = at_ref[0], at_ref[1], at_ref[2]

        def take(o, i, e):
            n, k = table.spots[spots[i]]
            return pltpu.make_async_copy(pieces[n].at[k + e], buf.at[o, i], sems.at[0, o, i])

        def put(o, i):
            return pltpu.make_async_copy(buf.at[o, i], outs[o].at[i], sems.at[1, o, i])

        every = [(o, i) for o in range(sides) for i in range(count)]
        for o, i in every:
            dx, dz = spots[i]
            take(o, i, want_refs[o][0, place_of(mx + dx, mz + dz, mc)]).start()

        for o, i in every:
            take(o, i, 0).wait()
            put(o, i).start()
        for o, i in every:
            put(o, i).wait()

    return pl.pallas_call(
        kernel,
        out_shape=[jax.ShapeDtypeStruct((count, *block), BF)] * sides,
        in_specs=[pl.BlockSpec(memory_space=pltpu.SMEM)] * (sides + 1)
        + [pl.BlockSpec(memory_space=pl.ANY)] * len(table.arrays),
        out_specs=[pl.BlockSpec(memory_space=pl.ANY)] * sides,
        scratch_shapes=[pltpu.VMEM((sides, count, *block), BF), pltpu.SemaphoreType.DMA((2, sides, count))],
        name="pick",
    )(*wants, position, *table.arrays)


def place_of(x, z, c):
    x = jnp.where(x >= NX, x - NX, x)
    z = jnp.where(z >= NZ, z - NZ, z)
    return x * (NZ * NC) + z * NC + c


def dot(a, b, ca, cb):
    return lax.dot_general(a, b, (((ca,), (cb,)), ((), ())), preferred_element_type=F32)


def forward(features, blocks, adjacency, cotangent, weight_in, weight_out, neighbor, counts, wanted, position, scale):
    nblocks, slots, rows, _ = adjacency.shape
    nodes, channels = features.shape
    hid = weight_in.shape[1]
    per = PER
    tile = per * rows
    steps = nblocks // per
    parts = len(blocks) - 4

    def kernel(
        nb_ref, cnt_ref, want_ref, at_ref, owned, given, given_third, given_p, given_q, *refs
    ):
        pieces = refs[:parts]
        adj, feat, cot, win, wout, gp_out, keep, send, src, joined, acc_in, acc_out, sems = refs[parts:]
        step = pl.program_id(0)
        mx, mz, mc = at_ref[0], at_ref[1], at_ref[2]

        def slot(b, s):
            return src.at[b, pl.ds(s * rows, rows)]

        def fetch(b, s):
            nb = nb_ref[b, s]
            live = s < cnt_ref[b]
            local = nb < nblocks
            q = jnp.maximum(nb - nblocks, 0)
            qx, qz, qc = q >> 4, (q >> 1) & 7, q & 1
            dx, dz = (qx - mx) & 3, (qz - mz) & 7
            far = dz == 4
            e = want_ref[0, q]

            def start(ref):
                pltpu.make_async_copy(ref, slot(b, s), sems.at[b, s]).start()

            inner = dx < 2
            at = jnp.where(inner, 2 * dx, 2 * (3 - dx)) + e
            hop = jnp.minimum(dz, NZ - dz)
            side = jnp.where(inner, 0, 2) + jnp.where(dz < 4, 1, 0)
            piece = jnp.where(inner, 0, 1) + jnp.where(hop == 0, 0, 4 * hop - 2 + jnp.where(far, 0, side - jnp.where(inner, 0, 1)))

            def start_piece(low, high):
                if high - low == 1:
                    start(pieces[low].at[at])
                    return
                mid = (low + high) // 2

                @pl.when(piece < mid)
                def _():
                    start_piece(low, mid)

                @pl.when(piece >= mid)
                def _():
                    start_piece(mid, high)

            def start_given():
                @pl.when(hop < 3)
                def _():
                    start(given.at[dx * 5 + jnp.where(dz < 3, dz, dz - 3)])

                @pl.when(hop == 3)
                def _():
                    start(given_third.at[dx * 2 + jnp.where(dz == 3, 0, 1)])

                @pl.when(jnp.logical_and(far, inner))
                def _():
                    start(given_p.at[at])

                @pl.when(jnp.logical_and(far, jnp.logical_not(inner)))
                def _():
                    start(given_q.at[at])

            @pl.when(live)
            def _():
                @pl.when(local)
                def _():
                    start(owned.at[pl.ds(pl.multiple_of(jnp.minimum(nb, nblocks - 1) * rows, rows), rows)])

                @pl.when(jnp.logical_not(local))
                def _():
                    @pl.when(qc == mc)
                    def _():
                        start_piece(0, parts)

                    @pl.when(qc != mc)
                    def _():
                        start_given()

            @pl.when(jnp.logical_not(live))
            def _():
                src[b, pl.ds(s * rows, rows)] = jnp.zeros((rows, channels), BF)

        @pl.when(step == 0)
        def _():
            @pl.loop(0, nblocks)
            def _(b):
                for s in range(slots):
                    fetch(b, s)

            acc_in[...] = jnp.zeros_like(acc_in)
            acc_out[...] = jnp.zeros_like(acc_out)

        for j in range(per):
            b = step * per + j
            for s in range(slots):

                @pl.when(s < cnt_ref[b])
                def _():
                    pltpu.make_async_copy(owned.at[pl.ds(0, rows)], slot(b, s), sems.at[b, s]).wait()

        for j in range(per):
            b = step * per + j
            agg = dot(adj[j, 0], src[b, :rows], 1, 0)
            for s in range(1, slots):
                agg += dot(adj[j, s], src[b, s * rows : (s + 1) * rows], 1, 0)
            joined[j * rows : (j + 1) * rows, :channels] = agg.astype(BF)
        joined[:, channels:] = feat[...]
        x = joined[...]
        g = cot[...]
        pre = dot(x, win[...], 1, 0)
        gh = dot(g, wout[...], 1, 1)
        sg = 0.5 * jnp.tanh(0.5 * pre) + 0.5
        silu = pre * sg
        hidden = silu.astype(BF)
        gp = (gh * (sg + silu * (1.0 - sg))).astype(BF)
        gp_out[...] = gp
        acc_in[...] += dot(x, gp, 0, 0)
        acc_out[...] += dot(hidden, g, 0, 0)

        @pl.when(step == steps - 1)
        def _():
            for i in range(NX * NZ):
                for ref, c in ((keep, mc), (send, 1 - mc)):
                    x = (i // NZ + mx) & 3
                    at = pl.multiple_of(((x * NZ + i % NZ) * NC + c) * 8, 8)
                    ref[i, :, :hid] = acc_in[pl.ds(at, 8), :] * scale
                    ref[i, :, hid:] = acc_out[pl.ds(at, 8), :] * scale

    smem = pl.BlockSpec(memory_space=pltpu.SMEM)
    whole = pl.BlockSpec(memory_space=pl.ANY)
    fixed = lambda a: pl.BlockSpec(a.shape, lambda i: (0,) * a.ndim, pipeline_mode=pl.Buffered(1))
    tiled = pl.BlockSpec((tile, channels), lambda i: (i, 0))
    part = (NX * NZ, 8, hid + channels)
    return pl.pallas_call(
        kernel,
        grid=(steps,),
        out_shape=[
            jax.ShapeDtypeStruct((nodes, hid), BF),
            jax.ShapeDtypeStruct(part, F32),
            jax.ShapeDtypeStruct(part, F32),
        ],
        in_specs=[smem] * 4
        + [whole] * (5 + parts)
        + [pl.BlockSpec((per, slots, rows, rows), lambda i: (i, 0, 0, 0)), tiled, tiled, fixed(weight_in), fixed(weight_out)],
        out_specs=[
            pl.BlockSpec((tile, hid), lambda i: (i, 0)),
            pl.BlockSpec(part, lambda i: (0, 0, 0)),
            pl.BlockSpec(part, lambda i: (0, 0, 0)),
        ],
        scratch_shapes=[
            pltpu.VMEM((nblocks, slots * rows, channels), BF),
            pltpu.VMEM((tile, 2 * channels), BF),
            pltpu.VMEM((2 * channels, hid), F32),
            pltpu.VMEM((hid, channels), F32),
            pltpu.SemaphoreType.DMA((nblocks, slots)),
        ],
        name="forward",
    )(neighbor, counts, wanted, position, features, *blocks, adjacency, features, cotangent, weight_in, weight_out)


def join_gradient(grad_preact, weight_in, half, before=()):
    nodes, hid = grad_preact.shape
    channels = weight_in.shape[0] // 2
    tile = nodes // 4

    def kernel(gp, win, *refs):
        ga, right = refs[-2:]
        gj = dot(gp[...], win[...], 1, 1)
        ga[...] = gj[:, :channels].astype(BF)
        right[...] = gj[:, channels:]

    return pl.pallas_call(
        kernel,
        grid=(2,),
        out_shape=[jax.ShapeDtypeStruct((nodes, channels), t) for t in (BF, F32)],
        in_specs=[
            pl.BlockSpec((tile, hid), lambda i: (i + 2 * half, 0)),
            pl.BlockSpec(weight_in.shape, lambda i: (0, 0), pipeline_mode=pl.Buffered(1)),
        ]
        + [pl.BlockSpec(memory_space=pl.ANY)] * len(before),
        out_specs=[pl.BlockSpec((tile, channels), lambda i: (i + 2 * half, 0))] * 2,
        input_output_aliases={2 + i: i for i in range(len(before))},
        name="joingrad",
    )(grad_preact, weight_in, *before)


def scatter_gradient(grad_aggregate, right, adjacency, neighbor, counts):
    nblocks, slots, rows, _ = adjacency.shape
    nodes, channels = right.shape
    per = PER
    steps = nblocks // per

    def kernel(nb_ref, cnt_ref, right_ref, ga, adj, out, acc, base, sem):
        step = pl.program_id(0)
        fill = pltpu.make_async_copy(right_ref, base, sem)

        @pl.when(step == 0)
        def _():
            fill.start()
            acc[...] = jnp.zeros_like(acc)

        for j in range(per):
            b = step * per + j
            for s in range(slots):
                nb = nb_ref[b, s]

                @pl.when(jnp.logical_and(s < cnt_ref[b], nb < nblocks))
                def _():
                    at = pl.ds(pl.multiple_of(jnp.minimum(nb, nblocks - 1) * rows, rows), rows)
                    acc[at, :] = acc[at, :] + dot(adj[j, s], ga[j * rows : (j + 1) * rows], 0, 0)

        @pl.when(step == steps - 1)
        def _():
            fill.wait()
            out[...] = (acc[...] + base[...]).astype(BF)

    smem = pl.BlockSpec(memory_space=pltpu.SMEM)
    return pl.pallas_call(
        kernel,
        grid=(steps,),
        out_shape=jax.ShapeDtypeStruct((nodes, channels), BF),
        in_specs=[
            smem,
            smem,
            pl.BlockSpec(memory_space=pl.ANY),
            pl.BlockSpec((per * rows, channels), lambda i: (i, 0)),
            pl.BlockSpec((per, slots, rows, rows), lambda i: (i, 0, 0, 0)),
        ],
        out_specs=pl.BlockSpec((nodes, channels), lambda i: (0, 0)),
        scratch_shapes=[
            pltpu.VMEM((nodes, channels), F32),
            pltpu.VMEM((nodes, channels), F32),
            pltpu.SemaphoreType.DMA(()),
        ],
        name="scattergrad",
    )(neighbor, counts, right, grad_aggregate, adjacency)


def reduce_terms(keep, send, hid):
    send = move(send, dc=1)
    keep = (keep + send).reshape(NX, NZ, *keep.shape[1:])
    there = keep[1:].astype(WIRE)
    parts = []
    for k in (1, 3, 2):
        parts.append(move(there[k - 1], dx=k))
    keep = (keep[0] + parts[0].astype(F32) + parts[1].astype(F32) + parts[2].astype(F32)).astype(WIRE)
    columns = [[place(x, z, c) for z in range(NZ)] for x in range(NX) for c in range(NC)]
    keep = lax.all_to_all(keep, "dom", 0, 0, axis_index_groups=columns).astype(F32).sum(0)
    parts = []
    for k in (1, 2, 3):
        parts.append(lax.ppermute(keep, "grp", [(i, i ^ k) for i in range(4)]))
    a, b, c = parts
    at = slice(0, hid), slice(hid, None)
    return [(keep[:, i] + a[:, i]) + (b[:, i] + c[:, i]) for i in at]


def layer(
    features, boundary_cache, adjacency, neighbor, counts, wanted, weight_in, weight_out, cotangent
):
    block_rows = adjacency.shape[2]
    channels = features.shape[1]
    hid = weight_in.shape[1]
    at = lax.axis_index("dom")
    position = jnp.stack([at // (NZ * NC), at // NC % NZ, at % NC]).astype(jnp.int32)
    exported = boundary_cache.astype(BF).reshape(-1, block_rows, channels)
    other = move(wanted, dc=1)
    near, first, third, far = gather_plane(exported)
    (given,) = pick(first, (other,), position)
    given = move(given, dc=1)
    (given_third,) = pick(third, (other,), position)
    given_third = move(given_third, dc=1)
    node_total = features.shape[0] * lax.axis_size("grp") * lax.axis_size("dom")
    scale = 1.0 / math.sqrt(node_total)
    grad_preact, keep, send = forward(
        features, (given, given_third, *far[2:], *near.arrays, *far[:2]), adjacency, cotangent, weight_in, weight_out,
        neighbor, counts, wanted, position, scale,
    )
    joined = join_gradient(grad_preact, weight_in, 0)
    grad_aggregate, right = join_gradient(grad_preact, weight_in, 1, joined)
    grad_features = scatter_gradient(grad_aggregate, right, adjacency, neighbor, counts)
    total = reduce_terms(keep, send, hid)
    return (grad_features, *total)


def solution(mesh):
    in_specs = (
        P(("grp", "dom"), None),
        P(("grp", "dom"), None),
        P(("grp", "dom"), None, None, None),
        P(("grp", "dom"), None),
        P(("grp", "dom")),
        P(("grp", "dom"), None),
        P(),
        P(),
        P(("grp", "dom"), None),
    )
    out_specs = (P(("grp", "dom"), None), P("dom", None), P("dom", None))
    return jax.shard_map(layer, mesh=mesh, in_specs=in_specs, out_specs=out_specs, check_vma=False)
```

```python
import math

import jax
import jax.numpy as jnp
from jax import lax
from jax.experimental import pallas as pl
from jax.experimental.pallas import tpu as pltpu
from jax.sharding import PartitionSpec as P


NX, NZ, NC = 4, 8, 2


def place(x, z, c):
    return (x % NX) * (NZ * NC) + (z % NZ) * NC + c


def move(a, dx=0, dz=0, dc=0):
    pairs = [
        (place(x, z, c), place(x + dx, z + dz, c ^ dc))
        for x in range(NX)
        for z in range(NZ)
        for c in range(NC)
    ]
    return lax.ppermute(a, "dom", pairs)


BF = jnp.bfloat16
F32 = jnp.float32
WIRE = jnp.bfloat16
PER = 6


class Table:
    def __init__(self):
        self.arrays, self.spots = [], {}

    def add(self, array, xs, dz):
        self.arrays.append(array)
        for i, dx in enumerate(xs):
            self.spots[dx % NX, dz % NZ] = (len(self.arrays) - 1, 2 * i)


def gather_plane(own):
    near, first, third = Table(), Table(), Table()

    def go(a, **step):
        return move(a, **step)

    c1, c2, c3 = go(own, dx=1), go(own, dx=-1), go(own, dx=2)
    p, q = jnp.concatenate([own, c2]), jnp.concatenate([c1, c3])
    px, qx = (0, 1), (-1, 2)
    for a, xs in ((p, px), (q, qx)):
        near.add(a, xs, 0)
        first.add(a, xs, 0)
    pp, pm, qp, qm = p, p, q, q
    for k in (1, 2, 3):
        pp, pm = go(pp, dz=1), go(pm, dz=-1)
        qp, qm = go(qp, dz=1), go(qm, dz=-1)
        for a, xs, dz in ((pp, px, -k), (pm, px, k), (qp, qx, -k), (qm, qx, k)):
            near.add(a, xs, dz)
            (first if k < 3 else third).add(a, xs, dz)
    p4 = go(pp, dz=1)
    given_p = move(p4, dc=1)
    q4 = go(qm, dz=-1)
    given_q = move(q4, dc=1)
    return near, first, third, (p4, q4, given_p, given_q)


def pick(table, wants, position):
    block = table.arrays[0].shape[1:]
    spots = sorted(table.spots)
    count, sides = len(spots), len(wants)

    def kernel(*refs):
        want_refs, at_ref, pieces = refs[:sides], refs[sides], refs[sides + 1 : -sides - 2]
        outs, buf, sems = refs[-sides - 2 : -2], refs[-2], refs[-1]
        mx, mz, mc = at_ref[0], at_ref[1], at_ref[2]

        def take(o, i, e):
            n, k = table.spots[spots[i]]
            return pltpu.make_async_copy(pieces[n].at[k + e], buf.at[o, i], sems.at[0, o, i])

        def put(o, i):
            return pltpu.make_async_copy(buf.at[o, i], outs[o].at[i], sems.at[1, o, i])

        every = [(o, i) for o in range(sides) for i in range(count)]
        for o, i in every:
            dx, dz = spots[i]
            take(o, i, want_refs[o][0, place_of(mx + dx, mz + dz, mc)]).start()

        for o, i in every:
            take(o, i, 0).wait()
            put(o, i).start()
        for o, i in every:
            put(o, i).wait()

    return pl.pallas_call(
        kernel,
        out_shape=[jax.ShapeDtypeStruct((count, *block), BF)] * sides,
        in_specs=[pl.BlockSpec(memory_space=pltpu.SMEM)] * (sides + 1)
        + [pl.BlockSpec(memory_space=pl.ANY)] * len(table.arrays),
        out_specs=[pl.BlockSpec(memory_space=pl.ANY)] * sides,
        scratch_shapes=[pltpu.VMEM((sides, count, *block), BF), pltpu.SemaphoreType.DMA((2, sides, count))],
        name="pick",
    )(*wants, position, *table.arrays)


def place_of(x, z, c):
    x = jnp.where(x >= NX, x - NX, x)
    z = jnp.where(z >= NZ, z - NZ, z)
    return x * (NZ * NC) + z * NC + c


def dot(a, b, ca, cb):
    return lax.dot_general(a, b, (((ca,), (cb,)), ((), ())), preferred_element_type=F32)


def forward(features, blocks, adjacency, cotangent, weight_in, weight_out, neighbor, counts, wanted, position, scale):
    nblocks, slots, rows, _ = adjacency.shape
    nodes, channels = features.shape
    hid = weight_in.shape[1]
    per = PER
    tile = per * rows
    steps = nblocks // per
    parts = len(blocks) - 4

    def kernel(
        nb_ref, cnt_ref, want_ref, at_ref, owned, given, given_third, given_p, given_q, *refs
    ):
        pieces = refs[:parts]
        adj, feat, cot, win, wout, gp_out, keep, send, src, joined, acc_in, acc_out, sems = refs[parts:]
        step = pl.program_id(0)
        mx, mz, mc = at_ref[0], at_ref[1], at_ref[2]

        def slot(b, s):
            return src.at[b, pl.ds(s * rows, rows)]

        def fetch(b, s):
            nb = nb_ref[b, s]
            live = s < cnt_ref[b]
            local = nb < nblocks
            q = jnp.maximum(nb - nblocks, 0)
            qx, qz, qc = q >> 4, (q >> 1) & 7, q & 1
            dx, dz = (qx - mx) & 3, (qz - mz) & 7
            far = dz == 4
            e = want_ref[0, q]

            def start(ref):
                pltpu.make_async_copy(ref, slot(b, s), sems.at[b, s]).start()

            inner = dx < 2
            at = jnp.where(inner, 2 * dx, 2 * (3 - dx)) + e
            hop = jnp.minimum(dz, NZ - dz)
            side = jnp.where(inner, 0, 2) + jnp.where(dz < 4, 1, 0)
            piece = jnp.where(inner, 0, 1) + jnp.where(hop == 0, 0, 4 * hop - 2 + jnp.where(far, 0, side - jnp.where(inner, 0, 1)))

            def start_piece(low, high):
                if high - low == 1:
                    start(pieces[low].at[at])
                    return
                mid = (low + high) // 2

                @pl.when(piece < mid)
                def _():
                    start_piece(low, mid)

                @pl.when(piece >= mid)
                def _():
                    start_piece(mid, high)

            def start_given():
                @pl.when(hop < 3)
                def _():
                    start(given.at[dx * 5 + jnp.where(dz < 3, dz, dz - 3)])

                @pl.when(hop == 3)
                def _():
                    start(given_third.at[dx * 2 + jnp.where(dz == 3, 0, 1)])

                @pl.when(jnp.logical_and(far, inner))
                def _():
                    start(given_p.at[at])

                @pl.when(jnp.logical_and(far, jnp.logical_not(inner)))
                def _():
                    start(given_q.at[at])

            @pl.when(live)
            def _():
                @pl.when(local)
                def _():
                    start(owned.at[pl.ds(pl.multiple_of(jnp.minimum(nb, nblocks - 1) * rows, rows), rows)])

                @pl.when(jnp.logical_not(local))
                def _():
                    @pl.when(qc == mc)
                    def _():
                        start_piece(0, parts)

                    @pl.when(qc != mc)
                    def _():
                        start_given()

            @pl.when(jnp.logical_not(live))
            def _():
                src[b, pl.ds(s * rows, rows)] = jnp.zeros((rows, channels), BF)

        @pl.when(step == 0)
        def _():
            @pl.loop(0, nblocks)
            def _(b):
                for s in range(slots):
                    fetch(b, s)

            acc_in[...] = jnp.zeros_like(acc_in)
            acc_out[...] = jnp.zeros_like(acc_out)

        for j in range(per):
            b = step * per + j
            for s in range(slots):

                @pl.when(s < cnt_ref[b])
                def _():
                    pltpu.make_async_copy(owned.at[pl.ds(0, rows)], slot(b, s), sems.at[b, s]).wait()

        for j in range(per):
            b = step * per + j
            agg = dot(adj[j, 0], src[b, :rows], 1, 0)
            for s in range(1, slots):
                agg += dot(adj[j, s], src[b, s * rows : (s + 1) * rows], 1, 0)
            joined[j * rows : (j + 1) * rows, :channels] = agg.astype(BF)
        joined[:, channels:] = feat[...]
        x = joined[...]
        g = cot[...]
        pre = dot(x, win[...], 1, 0)
        gh = dot(g, wout[...], 1, 1)
        sg = 0.5 * jnp.tanh(0.5 * pre) + 0.5
        silu = pre * sg
        hidden = silu.astype(BF)
        gp = (gh * (sg + silu * (1.0 - sg))).astype(BF)
        gp_out[...] = gp
        acc_in[...] += dot(x, gp, 0, 0)
        acc_out[...] += dot(hidden, g, 0, 0)

        @pl.when(step == steps - 1)
        def _():
            for i in range(NX * NZ):
                for ref, c in ((keep, mc), (send, 1 - mc)):
                    x = (i // NZ + mx) & 3
                    at = pl.multiple_of(((x * NZ + i % NZ) * NC + c) * 8, 8)
                    ref[i, :, :hid] = acc_in[pl.ds(at, 8), :] * scale
                    ref[i, :, hid:] = acc_out[pl.ds(at, 8), :] * scale

    smem = pl.BlockSpec(memory_space=pltpu.SMEM)
    whole = pl.BlockSpec(memory_space=pl.ANY)
    fixed = lambda a: pl.BlockSpec(a.shape, lambda i: (0,) * a.ndim, pipeline_mode=pl.Buffered(1))
    tiled = pl.BlockSpec((tile, channels), lambda i: (i, 0))
    part = (NX * NZ, 8, hid + channels)
    return pl.pallas_call(
        kernel,
        grid=(steps,),
        out_shape=[
            jax.ShapeDtypeStruct((nodes, hid), BF),
            jax.ShapeDtypeStruct(part, F32),
            jax.ShapeDtypeStruct(part, F32),
        ],
        in_specs=[smem] * 4
        + [whole] * (5 + parts)
        + [pl.BlockSpec((per, slots, rows, rows), lambda i: (i, 0, 0, 0)), tiled, tiled, fixed(weight_in), fixed(weight_out)],
        out_specs=[
            pl.BlockSpec((tile, hid), lambda i: (i, 0)),
            pl.BlockSpec(part, lambda i: (0, 0, 0)),
            pl.BlockSpec(part, lambda i: (0, 0, 0)),
        ],
        scratch_shapes=[
            pltpu.VMEM((nblocks, slots * rows, channels), BF),
            pltpu.VMEM((tile, 2 * channels), BF),
            pltpu.VMEM((2 * channels, hid), F32),
            pltpu.VMEM((hid, channels), F32),
            pltpu.SemaphoreType.DMA((nblocks, slots)),
        ],
        name="forward",
    )(neighbor, counts, wanted, position, features, *blocks, adjacency, features, cotangent, weight_in, weight_out)


def join_gradient(grad_preact, weight_in, begin, end, before=()):
    nodes, hid = grad_preact.shape
    channels = weight_in.shape[0] // 2
    tile = nodes // 4

    def kernel(gp, win, *refs):
        ga, right = refs[-2:]
        gj = dot(gp[...], win[...], 1, 1)
        ga[...] = gj[:, :channels].astype(BF)
        right[...] = gj[:, channels:]

    return pl.pallas_call(
        kernel,
        grid=(end - begin,),
        out_shape=[jax.ShapeDtypeStruct((nodes, channels), t) for t in (BF, F32)],
        in_specs=[
            pl.BlockSpec((tile, hid), lambda i: (i + begin, 0)),
            pl.BlockSpec(weight_in.shape, lambda i: (0, 0), pipeline_mode=pl.Buffered(1)),
        ]
        + [pl.BlockSpec(memory_space=pl.ANY)] * len(before),
        out_specs=[pl.BlockSpec((tile, channels), lambda i: (i + begin, 0))] * 2,
        input_output_aliases={2 + i: i for i in range(len(before))},
        name="joingrad",
    )(grad_preact, weight_in, *before)


def scatter_gradient(grad_aggregate, right, adjacency, neighbor, counts):
    nblocks, slots, rows, _ = adjacency.shape
    nodes, channels = right.shape
    per = PER
    steps = nblocks // per

    def kernel(nb_ref, cnt_ref, right_ref, ga, adj, out, acc, base, sem):
        step = pl.program_id(0)
        fill = pltpu.make_async_copy(right_ref, base, sem)

        @pl.when(step == 0)
        def _():
            fill.start()
            acc[...] = jnp.zeros_like(acc)

        for j in range(per):
            b = step * per + j
            for s in range(slots):
                nb = nb_ref[b, s]

                @pl.when(jnp.logical_and(s < cnt_ref[b], nb < nblocks))
                def _():
                    at = pl.ds(pl.multiple_of(jnp.minimum(nb, nblocks - 1) * rows, rows), rows)
                    acc[at, :] = acc[at, :] + dot(adj[j, s], ga[j * rows : (j + 1) * rows], 0, 0)

        @pl.when(step == steps - 1)
        def _():
            fill.wait()
            out[...] = (acc[...] + base[...]).astype(BF)

    smem = pl.BlockSpec(memory_space=pltpu.SMEM)
    return pl.pallas_call(
        kernel,
        grid=(steps,),
        out_shape=jax.ShapeDtypeStruct((nodes, channels), BF),
        in_specs=[
            smem,
            smem,
            pl.BlockSpec(memory_space=pl.ANY),
            pl.BlockSpec((per * rows, channels), lambda i: (i, 0)),
            pl.BlockSpec((per, slots, rows, rows), lambda i: (i, 0, 0, 0)),
        ],
        out_specs=pl.BlockSpec((nodes, channels), lambda i: (0, 0)),
        scratch_shapes=[
            pltpu.VMEM((nodes, channels), F32),
            pltpu.VMEM((nodes, channels), F32),
            pltpu.SemaphoreType.DMA(()),
        ],
        name="scattergrad",
    )(neighbor, counts, right, grad_aggregate, adjacency)


def reduce_terms(keep, send, hid):
    send = move(send, dc=1)
    keep = (keep + send).reshape(NX, NZ, *keep.shape[1:])
    there = keep[1:].astype(WIRE)
    parts = []
    for k in (1, 3, 2):
        parts.append(move(there[k - 1], dx=k))
    keep = (keep[0] + parts[0].astype(F32) + parts[1].astype(F32) + parts[2].astype(F32)).astype(WIRE)
    columns = [[place(x, z, c) for z in range(NZ)] for x in range(NX) for c in range(NC)]
    keep = lax.all_to_all(keep, "dom", 0, 0, axis_index_groups=columns).astype(F32).sum(0)
    parts = []
    for k in (1, 2, 3):
        parts.append(lax.ppermute(keep, "grp", [(i, i ^ k) for i in range(4)]))
    a, b, c = parts
    at = slice(0, hid), slice(hid, None)
    return [(keep[:, i] + a[:, i]) + (b[:, i] + c[:, i]) for i in at]


def layer(
    features, boundary_cache, adjacency, neighbor, counts, wanted, weight_in, weight_out, cotangent
):
    block_rows = adjacency.shape[2]
    channels = features.shape[1]
    hid = weight_in.shape[1]
    at = lax.axis_index("dom")
    position = jnp.stack([at // (NZ * NC), at // NC % NZ, at % NC]).astype(jnp.int32)
    exported = boundary_cache.astype(BF).reshape(-1, block_rows, channels)
    other = move(wanted, dc=1)
    near, first, third, far = gather_plane(exported)
    (given,) = pick(first, (other,), position)
    given = move(given, dc=1)
    (given_third,) = pick(third, (other,), position)
    given_third = move(given_third, dc=1)
    node_total = features.shape[0] * lax.axis_size("grp") * lax.axis_size("dom")
    scale = 1.0 / math.sqrt(node_total)
    grad_preact, keep, send = forward(
        features, (given, given_third, *far[2:], *near.arrays, *far[:2]), adjacency, cotangent, weight_in, weight_out,
        neighbor, counts, wanted, position, scale,
    )
    joined = join_gradient(grad_preact, weight_in, 0, 1)
    grad_aggregate, right = join_gradient(grad_preact, weight_in, 1, 4, joined)
    grad_features = scatter_gradient(grad_aggregate, right, adjacency, neighbor, counts)
    total = reduce_terms(keep, send, hid)
    return (grad_features, *total)


def solution(mesh):
    in_specs = (
        P(("grp", "dom"), None),
        P(("grp", "dom"), None),
        P(("grp", "dom"), None, None, None),
        P(("grp", "dom"), None),
        P(("grp", "dom")),
        P(("grp", "dom"), None),
        P(),
        P(),
        P(("grp", "dom"), None),
    )
    out_specs = (P(("grp", "dom"), None), P("dom", None), P("dom", None))
    return jax.shard_map(layer, mesh=mesh, in_specs=in_specs, out_specs=out_specs, check_vma=False)
```
